32 devices in a mesh: groups: 2 (over y), expert: 4 (over z), tensor: 4 (over x, core).
Axes of the slice: x: 2, y: 2, z: 4, core: 2. Of those that a mesh axis runs over, the one named last changes fastest.
Arguments:
- tokens: bfloat16 [1280, 3584], P(('groups', 'expert')), parts along dimension 0, may hold values from -6 to 6
- affinity: float32 [1280, 8], P(('groups', 'expert')), parts along dimension 0, may hold values from 0.05 to 1
- expert_ids: int32 [1280, 8], P(('groups', 'expert')), parts along dimension 0, may hold values from 0 to 255, as said below
- capacity: int32 [8], P('groups'), parts along dimension 0, may hold values from 4 to 8
- routed_gate: bfloat16 [4, 3584, 1024], P('expert', None, 'tensor'), may hold values from -0.09375 to 0.09375
- routed_up: bfloat16 [4, 3584, 1024], P('expert', None, 'tensor'), may hold values from -0.09375 to 0.09375
- routed_down: bfloat16 [4, 1024, 3584], P('expert', 'tensor'), may hold values from -0.1875 to 0.1875
- shared_gate: bfloat16 [3584, 2048], P('expert', 'tensor'), may hold values from -0.09375 to 0.09375
- shared_up: bfloat16 [3584, 2048], P('expert', 'tensor'), may hold values from -0.09375 to 0.09375
- shared_down_t: bfloat16 [3584, 2048], P('expert', 'tensor'), may hold values from -0.125 to 0.125
Outputs:
- mixed: bfloat16 [1280, 3584], P(('groups', 'expert'), 'tensor'), parts along dimension 0
The draws below stay inside these ranges and needn't reach their ends.
There are 2 independent parts, one for each index of `groups`. The reference program is written for one: setup_inputs(seed, part) draws one part's arguments, and reference() takes and returns one part's arrays. A program takes and returns all parts, laid end to end along the dimension named above; an argument that names none is the same for every part. Nothing has to cross between parts.
Inputs may be any that keep to these rules, and one draw needn't show every extreme that they name: `expert_ids`: each row names 8 different experts.
All inputs are finite; a program needn't handle non-finite values.
Results may differ from the reference program's by a relative error of at most 0.014.
Values may be sent and summed in bfloat16 or wider, within the bound.
A program may use at most 64 MiB of HBM per device.

```python
import jax
import jax.numpy as jnp
from jax import lax

D = 3584
H = 1024
S = 2048
EXPERTS = 256
TOP = 8
TOK_DEV = 160
CAP = 8
WINDOW = 4
TOKENS = 640
N_TENSOR = 4


def chosen_expert(key):
    return jax.random.randint(jax.random.fold_in(key, 11), (), 0, WINDOW)


def block_order(block_key):
    return jax.random.permutation(block_key, TOK_DEV)


def draw_expert_ids(key, part):
    favoured = chosen_expert(key)
    base_score = jax.random.randint(jax.random.fold_in(key, 1), (TOKENS, EXPERTS), 0, 65536)
    popularity = jax.random.randint(jax.random.fold_in(key, 2), (EXPERTS,), 0, 5)
    coin_rows = jax.random.randint(jax.random.fold_in(key, 3), (TOKENS,), 0, 4) == 0
    block_keys = jax.random.split(jax.random.fold_in(key, 4), TOKENS // TOK_DEV)
    orders = jax.vmap(block_order)(block_keys)
    ranks = jnp.argsort(orders, axis=1)
    forced = (ranks < CAP).reshape(TOKENS) | coin_rows
    columns = jnp.arange(EXPERTS, dtype=jnp.int32)
    boost = jnp.where(forced[:, None] & (columns[None, :] == favoured), 262144, 0)
    score = base_score + popularity[None, :] * 4096 + boost
    keyed = score * EXPERTS + columns[None, :]
    return lax.top_k(keyed, TOP)[1].astype(jnp.int32)


def draw_capacity(key, part):
    favoured = chosen_expert(key)
    values = jax.random.randint(jax.random.fold_in(key, 5), (WINDOW,), CAP // 2, CAP + 1)
    return jnp.where(jnp.arange(WINDOW) == favoured, CAP, values).astype(jnp.int32)


def block_levels(key, extent, pieces, least, top_value):
    gain, own = 1.0, jax.random.fold_in(key, 6)
    for axis_at, blocks in pieces:
        draws = jnp.exp(jax.random.uniform(jax.random.fold_in(own, axis_at), (blocks,), jnp.float32, least / len(pieces), top_value / len(pieces)))
        gain = gain * jnp.repeat(draws, extent[axis_at] // blocks).reshape([-1 if axis == axis_at else 1 for axis in range(len(extent))])
    return gain


def centred(own_key, shape, scale, most, shards=(), kind=jnp.bfloat16):
    gain = block_levels(own_key, shape, shards, -0.22, 0.18) if shards else 1.0
    values = jax.random.normal(own_key, shape, jnp.float32) * scale * gain
    return jnp.minimum(jnp.maximum(values, -most), most).astype(kind)


def setup_inputs(seed: int = 0, part: int = 0) -> dict:
    key_list = jax.random.split(jax.random.key(seed), 11)
    part_keys = jax.random.split(jax.random.fold_in(key_list[10], part), 11)
    tokens = centred(part_keys[0], (TOKENS, D), 1.0, 6.0, ((0, 4),))
    affinity = jnp.clip(0.05 + 0.95 * jax.random.uniform(part_keys[1], (TOKENS, TOP), jnp.float32) ** block_levels(part_keys[1], (TOKENS, TOP), ((0, 4),), -0.2, 0.2), 0.05, 1.0)
    expert_ids = draw_expert_ids(jax.random.fold_in(jax.random.fold_in(key_list[10], part), 71), part)
    capacity = draw_capacity(jax.random.fold_in(jax.random.fold_in(key_list[10], part), 71), part)
    routed_gate = centred(key_list[4], (WINDOW, D, H), D ** -0.5, 0.09375, ((0, 4), (2, 4)))
    routed_up = centred(key_list[5], (WINDOW, D, H), D ** -0.5, 0.09375, ((0, 4), (2, 4)))
    routed_down = centred(key_list[6], (WINDOW, H, D), H ** -0.5, 0.1875, ((0, 4), (1, 4)))
    shared_gate = centred(key_list[7], (D, S), D ** -0.5, 0.09375, ((0, 4), (1, 4)))
    shared_up = centred(key_list[8], (D, S), D ** -0.5, 0.09375, ((0, 4), (1, 4)))
    shared_down_t = centred(key_list[9], (D, S), S ** -0.5, 0.125, ((0, 4), (1, 4)))
    return dict(tokens=tokens, affinity=affinity, expert_ids=expert_ids, capacity=capacity, routed_gate=routed_gate, routed_up=routed_up, routed_down=routed_down, shared_gate=shared_gate, shared_up=shared_up, shared_down_t=shared_down_t)


def reference(tokens, affinity, expert_ids, capacity, routed_gate, routed_up, routed_down, shared_gate, shared_up, shared_down_t):
    window = capacity.shape[0]
    blocks = tokens.shape[0] // TOK_DEV
    columns = jnp.arange(window, dtype=jnp.int32)
    matches = (expert_ids[:, :, None] == columns[None, None, :]).astype(jnp.float32)
    hit_mask = jnp.sum(matches, axis=1)
    route_weight = 2.5 * jnp.sum(affinity[:, :, None] * matches, axis=1) / jnp.sum(affinity, axis=1, keepdims=True)
    per_block = hit_mask.reshape(blocks, TOK_DEV, window)
    slot_index = jnp.cumsum(per_block, axis=1) - per_block
    kept_mask = per_block * (slot_index < capacity[None, None, :].astype(jnp.float32)).astype(jnp.float32)
    levels = jnp.arange(CAP).astype(jnp.float32)
    kept_turned = jnp.transpose(kept_mask, (0, 2, 1))
    slot_turned = jnp.transpose(slot_index, (0, 2, 1))
    placement = kept_turned[:, :, None, :] * (slot_turned[:, :, None, :] == levels[None, None, :, None]).astype(jnp.float32)
    positions = jnp.arange(TOK_DEV).astype(jnp.float32)
    local_index = jnp.sum(placement * positions[None, None, None, :], axis=3)
    valid_rows = jnp.sum(placement, axis=3)
    weight_block = jnp.transpose(route_weight.reshape(blocks, TOK_DEV, window), (0, 2, 1))
    slot_weight = jnp.sum(placement * weight_block[:, :, None, :], axis=3)
    offsets = (jnp.arange(blocks) * TOK_DEV).astype(jnp.float32)
    row_index = (local_index + offsets[:, None, None]).astype(jnp.int32)

    def expert_rows(arranged):
        return jnp.transpose(arranged, (1, 0, 2)).reshape(window, -1)

    def one_expert(routed_sum, inputs):
        rows_index, rows_valid, rows_weight, gate_weight, up_weight, down_weight = inputs
        gathered = tokens[rows_index] * rows_valid[:, None].astype(jnp.bfloat16)
        gate_rows = jnp.dot(gathered, gate_weight, preferred_element_type=jnp.float32)
        up_rows = jnp.dot(gathered, up_weight, preferred_element_type=jnp.float32)
        activated = (jax.nn.silu(gate_rows) * up_rows).astype(jnp.bfloat16)
        grouped = activated.reshape(activated.shape[0], N_TENSOR, -1).astype(jnp.float32)
        down_groups = down_weight.reshape(N_TENSOR, -1, down_weight.shape[1]).astype(jnp.float32)
        group_parts = jnp.einsum("rgh,ghd->grd", grouped, down_groups)
        rounded = lax.optimization_barrier(group_parts.astype(jnp.bfloat16))
        expert_out = jnp.sum(rounded.astype(jnp.float32), axis=0)
        routed_sum = routed_sum.at[rows_index].add(expert_out * rows_weight[:, None])
        return routed_sum, None

    inputs_all = (expert_rows(row_index), expert_rows(valid_rows), expert_rows(slot_weight), routed_gate, routed_up, routed_down)
    start_sum = jnp.zeros((tokens.shape[0], tokens.shape[1]), jnp.float32)
    routed_total = lax.scan(one_expert, start_sum, inputs_all)[0]
    shared_gate_rows = jnp.dot(tokens, shared_gate, preferred_element_type=jnp.float32)
    shared_up_rows = jnp.dot(tokens, shared_up, preferred_element_type=jnp.float32)
    shared_hidden = (jax.nn.silu(shared_gate_rows) * shared_up_rows).astype(jnp.bfloat16)
    shared_out = jnp.dot(shared_hidden, shared_down_t.T, preferred_element_type=jnp.float32)
    return (routed_total + shared_out).astype(jnp.bfloat16)
```

```python
import jax
import jax.numpy as jnp
from jax import lax
from jax.sharding import PartitionSpec as P

CAP = 8


def routing_tables(affinity, expert_ids, capacity):
    window = capacity.shape[0]
    tok_rows = expert_ids.shape[0]
    columns = jnp.arange(window, dtype=jnp.int32)
    matches = (expert_ids[:, :, None] == columns[None, None, :]).astype(jnp.float32)
    hit_mask = jnp.sum(matches, axis=1)
    route_weight = (
        2.5
        * jnp.sum(affinity[:, :, None] * matches, axis=1)
        / jnp.sum(affinity, axis=1, keepdims=True)
    )
    earlier = jnp.tril(jnp.ones((tok_rows, tok_rows), jnp.float32), -1)
    slot_index = jnp.dot(earlier, hit_mask, precision=lax.Precision.HIGHEST)
    kept_mask = hit_mask * (slot_index < capacity[None, :].astype(jnp.float32)).astype(jnp.float32)
    levels = jnp.arange(CAP, dtype=jnp.float32)
    placement = kept_mask.T[:, None, :] * (
        slot_index.T[:, None, :] == levels[None, :, None]
    ).astype(jnp.float32)
    return (placement, route_weight)


def local(
    tokens,
    affinity,
    expert_ids,
    capacity,
    routed_gate,
    routed_up,
    routed_down,
    shared_gate,
    shared_up,
    shared_down_t,
):
    columns = lax.all_to_all(tokens, "expert", split_axis=1, concat_axis=0, tiled=True)
    gate_part = jnp.dot(columns, shared_gate, preferred_element_type=jnp.float32)
    up_part = jnp.dot(columns, shared_up, preferred_element_type=jnp.float32)
    both_part = jnp.concatenate([gate_part, up_part], axis=1).astype(jnp.bfloat16)
    both_rows = lax.psum_scatter(both_part, "expert", scatter_dimension=0, tiled=True).astype(
        jnp.float32
    )
    placement, route_weight = routing_tables(affinity, expert_ids, capacity)
    placement_half = placement.astype(jnp.bfloat16)
    outgoing = jnp.einsum(
        "ect,td->ecd", placement_half, tokens, preferred_element_type=jnp.float32
    ).astype(jnp.bfloat16)
    received = lax.all_to_all(outgoing, "expert", split_axis=0, concat_axis=0, tiled=True)
    flat_rows = received.reshape(-1, received.shape[-1])
    gate_rows = jnp.dot(flat_rows, routed_gate[0], preferred_element_type=jnp.float32)
    up_rows = jnp.dot(flat_rows, routed_up[0], preferred_element_type=jnp.float32)
    activated = (jax.nn.silu(gate_rows) * up_rows).astype(jnp.bfloat16)
    partial_out = jnp.dot(activated, routed_down[0], preferred_element_type=jnp.float32)
    partial_out = partial_out.reshape(received.shape[0], received.shape[1], partial_out.shape[-1])
    owner_total = lax.psum_scatter(
        partial_out.astype(jnp.bfloat16), "tensor", scatter_dimension=2, tiled=True
    ).astype(jnp.float32)
    back_rows = lax.all_to_all(
        owner_total.astype(jnp.bfloat16), "expert", split_axis=0, concat_axis=0, tiled=True
    ).astype(owner_total.dtype)
    hidden_units = shared_gate.shape[1]
    shared_hidden = (
        jax.nn.silu(both_rows[:, :hidden_units]) * both_rows[:, hidden_units:]
    ).astype(jnp.bfloat16)
    hidden_all = lax.all_gather(shared_hidden, "expert", axis=0, tiled=True)
    shared_cols = lax.dot_general(
        hidden_all, shared_down_t, (((1,), (1,)), ((), ())), preferred_element_type=jnp.float32
    ).astype(jnp.bfloat16)
    shared_out = lax.all_to_all(shared_cols, "expert", split_axis=0, concat_axis=1, tiled=True)
    weighted = placement * route_weight.T[:, None, :]
    routed_out = jnp.einsum("ect,ecd->td", weighted, back_rows, precision=lax.Precision.HIGHEST)
    summed = lax.psum_scatter(
        shared_out.astype(jnp.bfloat16), "tensor", scatter_dimension=1, tiled=True
    ).astype(jnp.float32)
    mixed_out = summed + routed_out
    return mixed_out.astype(jnp.bfloat16)


def solution(mesh):
    in_specs = (
        P(("groups", "expert"), None),
        P(("groups", "expert"), None),
        P(("groups", "expert"), None),
        P("groups"),
        P("expert", None, "tensor"),
        P("expert", None, "tensor"),
        P("expert", "tensor", None),
        P("expert", "tensor"),
        P("expert", "tensor"),
        P("expert", "tensor"),
    )
    out_specs = P(("groups", "expert"), "tensor")
    return jax.shard_map(local, mesh=mesh, in_specs=in_specs, out_specs=out_specs, check_vma=False)
```

```python
import functools

import jax
import jax.numpy as jnp
from jax import lax
from jax.experimental import pallas as pl
from jax.experimental.pallas import tpu as pltpu
from jax.sharding import PartitionSpec as P

CAP = 8


def routing_tables(affinity, expert_ids, capacity):
    window = capacity.shape[0]
    tok_rows = expert_ids.shape[0]
    columns = jnp.arange(window, dtype=jnp.int32)
    matches = (expert_ids[:, :, None] == columns[None, None, :]).astype(jnp.float32)
    hit_mask = jnp.sum(matches, axis=1)
    route_weight = (
        2.5
        * jnp.sum(affinity[:, :, None] * matches, axis=1)
        / jnp.sum(affinity, axis=1, keepdims=True)
    )
    earlier = jnp.tril(jnp.ones((tok_rows, tok_rows), jnp.float32), -1)
    slot_index = jnp.dot(earlier, hit_mask, precision=lax.Precision.HIGHEST)
    kept_mask = hit_mask * (slot_index < capacity[None, :].astype(jnp.float32)).astype(jnp.float32)
    levels = jnp.arange(CAP, dtype=jnp.float32)
    placement = kept_mask.T[:, None, :] * (
        slot_index.T[:, None, :] == levels[None, :, None]
    ).astype(jnp.float32)
    return (placement, route_weight)


def local(
    tokens,
    affinity,
    expert_ids,
    capacity,
    routed_gate,
    routed_up,
    routed_down,
    shared_gate,
    shared_up,
    shared_down_t,
):
    gathered_gate, gathered_up, gathered_down = (
        lax.all_gather(shared_gate, "expert", axis=0, tiled=True),
        lax.all_gather(shared_up, "expert", axis=0, tiled=True),
        lax.all_gather(shared_down_t, "expert", axis=0, tiled=True),
    )
    placement, route_weight = routing_tables(affinity, expert_ids, capacity)
    placement_half = placement.astype(jnp.bfloat16)
    outgoing = jnp.einsum(
        "ect,td->ecd", placement_half, tokens, preferred_element_type=jnp.float32
    ).astype(jnp.bfloat16)
    received = lax.all_to_all(outgoing, "expert", split_axis=0, concat_axis=0, tiled=True)
    flat_rows = received.reshape(-1, received.shape[-1])
    gate_rows = jnp.dot(flat_rows, routed_gate[0], preferred_element_type=jnp.float32)
    up_rows = jnp.dot(flat_rows, routed_up[0], preferred_element_type=jnp.float32)
    activated = (jax.nn.silu(gate_rows) * up_rows).astype(jnp.bfloat16)
    partial_out = jnp.dot(activated, routed_down[0], preferred_element_type=jnp.float32)
    partial_out = partial_out.reshape(received.shape[0], received.shape[1], partial_out.shape[-1])
    owner_total = lax.psum_scatter(
        partial_out.astype(jnp.bfloat16), "tensor", scatter_dimension=2, tiled=True
    ).astype(jnp.float32)
    back_rows = lax.all_to_all(
        owner_total.astype(jnp.bfloat16), "expert", split_axis=0, concat_axis=0, tiled=True
    ).astype(owner_total.dtype)
    shared_gate_rows = jnp.dot(tokens, gathered_gate, preferred_element_type=jnp.float32)
    shared_up_rows = jnp.dot(tokens, gathered_up, preferred_element_type=jnp.float32)
    shared_hidden = (jax.nn.silu(shared_gate_rows) * shared_up_rows).astype(jnp.bfloat16)
    shared_out = lax.dot_general(
        shared_hidden, gathered_down, (((1,), (1,)), ((), ())), preferred_element_type=jnp.float32
    )
    weighted = placement * route_weight.T[:, None, :]
    routed_out = jnp.einsum("ect,ecd->td", weighted, back_rows, precision=lax.Precision.HIGHEST)
    summed = lax.psum_scatter(
        shared_out.astype(jnp.bfloat16), "tensor", scatter_dimension=1, tiled=True
    ).astype(jnp.float32)
    mixed_out = summed + routed_out
    return mixed_out.astype(jnp.bfloat16)


MESH = pl.DeviceIdType.MESH
F32 = jnp.float32
BF16 = jnp.bfloat16


def remote(src, dst, send_sem, recv_sem, **device):
    return pltpu.make_async_remote_copy(
        src_ref=src,
        dst_ref=dst,
        send_sem=send_sem,
        recv_sem=recv_sem,
        device_id=device,
        device_id_type=MESH,
    )


def fused_kernel(
    n_exp, n_ten,
    tok_any, aff_ref, ids_ref, cap_ref, rg_any, ru_any, rd_any, sg_any, su_any, sd_any,
    out_ref,
    tok, wgu, wdn, rgw, ruw, rdw, xall, gown, gsend, gin, hall, weights,
    rout, rin, ys, yin, yb, back, acc, osend, oin, rsend, rfin, routed,
    lsem, ax_s, ax_r, af_s, af_r, bx_s, bx_r, bf_s, bf_r, c_s, c_r, h_s, h_r,
    y_s, y_r, k_s, k_r, o_s, o_r, t_s, t_r,
):
    e, t = lax.axis_index("expert"), lax.axis_index("tensor")
    core = lax.rem(t, 2)
    partner = t + 1 - 2 * core
    rows, width = tok.shape
    cols = width // n_exp
    half = rows // 2
    half_width = width // 2
    hidden = hall.shape[2]
    others = range(1, n_exp)

    def up(k):
        return lax.rem(e + k, n_exp)

    def down(k):
        return lax.rem(e - k + n_exp, n_exp)

    def span(index, size, unit=128):
        return pl.ds(pl.multiple_of(index * size, unit), size)

    loads = [
        pltpu.make_async_copy(tok_any, tok, lsem.at[0]),
        pltpu.make_async_copy(sg_any, wgu.at[:, pl.ds(0, hidden)], lsem.at[1]),
        pltpu.make_async_copy(su_any, wgu.at[:, pl.ds(hidden, hidden)], lsem.at[2]),
        pltpu.make_async_copy(rg_any.at[0], rgw, lsem.at[3]),
        pltpu.make_async_copy(ru_any.at[0], ruw, lsem.at[4]),
        pltpu.make_async_copy(rd_any.at[0], rdw, lsem.at[5]),
        pltpu.make_async_copy(sd_any, wdn, lsem.at[6]),
    ]
    for load in loads:
        load.start()

    barrier = pltpu.get_barrier_semaphore()
    for k in others:
        pl.semaphore_signal(barrier, inc=1, device_id={"expert": up(k)}, device_id_type=MESH)
    for k in range(1, n_ten):
        pl.semaphore_signal(
            barrier, inc=1, device_id={"tensor": lax.rem(t + k, n_ten)}, device_id_type=MESH
        )

    @pl.when(e != t)
    def _():
        pl.semaphore_signal(
            barrier, inc=1, device_id={"expert": t, "tensor": e}, device_id_type=MESH
        )

    pl.semaphore_wait(barrier, n_exp + n_ten - 2 + (e != t).astype(jnp.int32))

    mine = span(core, half, 16)
    a_copy = {}
    for k in others:
        a_copy[k] = remote(
            tok_any.at[mine, span(up(k), cols)], xall.at[e, mine, :],
            ax_s.at[k - 1], ax_r.at[k - 1], expert=up(k),
        )
        a_copy[k].start()

    lanes = n_exp * CAP
    column = lax.broadcasted_iota(jnp.int32, (rows, lanes), 1)
    expert_of, level = column // CAP, lax.rem(column, CAP)
    ids, aff = ids_ref[...], aff_ref[...]
    hit = jnp.zeros((rows, lanes), F32)
    chosen = jnp.zeros((rows, lanes), F32)
    for k in range(ids.shape[1]):
        match = (ids[:, k : k + 1] == expert_of).astype(F32)
        hit += match
        chosen += match * aff[:, k : k + 1]
    share = 2.5 * chosen / jnp.sum(aff, axis=1, keepdims=True)
    earlier = (
        lax.broadcasted_iota(jnp.int32, (rows, rows), 1)
        < lax.broadcasted_iota(jnp.int32, (rows, rows), 0)
    ).astype(BF16)
    slot = jnp.dot(earlier, hit.astype(BF16), preferred_element_type=F32)
    limit = jnp.zeros((rows, lanes), jnp.int32)
    for k in range(n_exp):
        limit = jnp.where(expert_of == k, cap_ref[k], limit)
    placed = (
        hit * (slot < limit.astype(F32)).astype(F32) * (slot == level.astype(F32)).astype(F32)
    )
    weights[...] = placed * share
    loads[0].wait()
    chosen_rows = jnp.dot(
        jnp.transpose(placed).astype(BF16), tok[...], preferred_element_type=F32
    ).astype(BF16).astype(F32)
    for k in range(n_exp):
        rout[k] = chosen_rows[k * CAP : (k + 1) * CAP].astype(BF16)
    side = span(core, half_width)
    b_copy = {}
    for k in others:
        b_copy[k] = remote(
            rout.at[up(k), :, side], rin.at[e, :, side],
            bx_s.at[k - 1], bx_r.at[k - 1], expert=up(k),
        )
        b_copy[k].start()
    rin[e] = rout[e]

    order = [k for k in others if k != n_exp // 2] + [n_exp // 2]
    af_copy, bf_copy = {}, {}
    for k in order:
        a_copy[k].wait_recv()
        af_copy[k] = remote(
            xall.at[down(k), mine, :], xall.at[down(k), mine, :],
            af_s.at[k - 1], af_r.at[k - 1], tensor=partner,
        )
        af_copy[k].start()
    loads[1].wait()
    loads[2].wait()
    c_copy = {}
    for k in order:
        af_copy[k].wait_recv()
        gsend[k - 1] = jnp.dot(
            xall[down(k)], wgu[...], preferred_element_type=F32
        ).astype(BF16)
        c_copy[k] = remote(
            gsend.at[k - 1], gin.at[k - 1], c_s.at[k - 1], c_r.at[k - 1], expert=down(k)
        )
        c_copy[k].start()
    for k in order:
        b_copy[k].wait_recv()
        bf_copy[k] = remote(
            rin.at[down(k), :, side], rin.at[down(k), :, side],
            bf_s.at[k - 1], bf_r.at[k - 1], tensor=partner,
        )
        bf_copy[k].start()
    gown[...] = jnp.dot(tok[:, span(e, cols)], wgu[...], preferred_element_type=F32)

    for load in loads[3:]:
        load.wait()
    for k in order:
        bf_copy[k].wait_recv()
    flat = jnp.concatenate([rin[k].astype(F32) for k in range(n_exp)], axis=0).astype(BF16)
    gate = jnp.dot(flat, rgw[...], preferred_element_type=F32)
    upper = jnp.dot(flat, ruw[...], preferred_element_type=F32)
    act = (gate * (1.0 / (1.0 + jnp.exp(-gate))) * upper).astype(BF16)
    ys[...] = jnp.dot(act, rdw[...], preferred_element_type=F32).astype(BF16)
    y_copy = {}
    part = width // n_ten
    for k in range(1, n_ten):
        to = lax.rem(t + k, n_ten)
        y_copy[k] = remote(
            ys.at[:, span(to, part)], yin.at[k - 1], y_s.at[k - 1], y_r.at[k - 1], tensor=to
        )
        y_copy[k].start()

    both = gown[...]
    for k in order:
        c_copy[k].wait_recv()
        both = both + gin[k - 1].astype(F32)
    gate = both[:, :hidden]
    hall[e] = (gate * (1.0 / (1.0 + jnp.exp(-gate))) * both[:, hidden:]).astype(BF16)
    h_copy = {}
    for k in others:
        h_copy[k] = remote(
            hall.at[e], hall.at[e], h_s.at[k - 1], h_r.at[k - 1], expert=up(k)
        )
        h_copy[k].start()

    total = ys[:, span(t, part)].astype(F32)
    for k in range(1, n_ten):
        y_copy[k].wait_recv()
        total = total + yin[k - 1].astype(F32)
    for k in range(n_exp):
        yb[k] = total[k * CAP : (k + 1) * CAP].astype(BF16)
    k_copy = {}
    for k in others:
        k_copy[k] = remote(
            yb.at[up(k)], back.at[e], k_s.at[k - 1], k_r.at[k - 1], expert=up(k)
        )
        k_copy[k].start()
    back[e] = yb[e]

    for k in order:
        h_copy[k].wait_recv()

    def product(index):
        return lax.dot_general(
            hall[index], wdn[...], (((1,), (1,)), ((), ())), preferred_element_type=F32
        )

    o_copy = []
    bits = n_ten.bit_length() - 1
    place = 0
    for s in range(bits):
        bit = lax.rem(t // (1 << s), 2)
        low = lax.rem(t, 1 << s)
        peer = t + (1 - 2 * bit) * (1 << s)
        count = n_ten >> (s + 1)
        copies = []
        for i in range(count):
            sent = (2 * i + 1 - bit) * (1 << s) + low
            osend[place + i] = (product(sent) if s == 0 else acc[sent]).astype(BF16)
            copy = remote(
                osend.at[place + i], oin.at[place + i],
                o_s.at[place + i], o_r.at[place + i], tensor=peer,
            )
            copy.start()
            copies.append(copy)
        if s == 0:
            for i in range(count):
                kept = 2 * i + bit
                acc[kept] = product(kept)
        for i in range(count):
            kept = (2 * i + bit) * (1 << s) + low
            copies[i].wait_recv()
            acc[kept] = acc[kept] + oin[place + i].astype(F32)
        o_copy += copies
        place += count
    final = remote(rsend, rfin, t_s, t_r, expert=t, tensor=e)

    @pl.when(e != t)
    def _():
        rsend[...] = acc[t].astype(BF16)
        final.start()

    @pl.when(e == t)
    def _():
        rfin[...] = acc[t].astype(BF16)

    for k in order:
        k_copy[k].wait_recv()
    rows_back = jnp.concatenate([back[k].astype(F32) for k in range(n_exp)], axis=0)
    routed[...] = jnp.dot(
        weights[...], rows_back, preferred_element_type=F32, precision=lax.Precision.HIGHEST
    )

    @pl.when(e != t)
    def _():
        final.wait()

    out_ref[...] = (rfin[...].astype(F32) + routed[...]).astype(BF16)
    for group in (a_copy, af_copy, b_copy, bf_copy, c_copy, h_copy, y_copy, k_copy):
        for copy in group.values():
            copy.wait_send()
    for copy in o_copy:
        copy.wait_send()


def fused(n_exp, n_ten, *args):
    tokens, affinity, expert_ids, capacity, rg, ru, rd, sg, su, sd = args
    rows, width = tokens.shape
    hidden = sg.shape[1]
    cols, part = width // n_exp, width // n_ten
    any_spec = pl.BlockSpec(memory_space=pl.ANY)
    vmem = pl.BlockSpec(memory_space=pltpu.VMEM)
    scratch = [
        pltpu.VMEM((rows, width), BF16),
        pltpu.VMEM((cols, 2 * hidden), BF16),
        pltpu.VMEM((cols, hidden), BF16),
        pltpu.VMEM(rg.shape[1:], BF16),
        pltpu.VMEM(ru.shape[1:], BF16),
        pltpu.VMEM(rd.shape[1:], BF16),
        pltpu.VMEM((n_exp, rows, cols), BF16),
        pltpu.VMEM((rows, 2 * hidden), F32),
        pltpu.VMEM((n_exp - 1, rows, 2 * hidden), BF16),
        pltpu.VMEM((n_exp - 1, rows, 2 * hidden), BF16),
        pltpu.VMEM((n_exp, rows, hidden), BF16),
        pltpu.VMEM((rows, n_exp * CAP), F32),
        pltpu.VMEM((n_exp, CAP, width), BF16),
        pltpu.VMEM((n_exp, CAP, width), BF16),
        pltpu.VMEM((n_exp * CAP, width), BF16),
        pltpu.VMEM((n_ten - 1, n_exp * CAP, part), BF16),
        pltpu.VMEM((n_exp, CAP, part), BF16),
        pltpu.VMEM((n_exp, CAP, part), BF16),
        pltpu.VMEM((n_ten, rows, part), F32),
        pltpu.VMEM((n_ten - 1, rows, part), BF16),
        pltpu.VMEM((n_ten - 1, rows, part), BF16),
        pltpu.VMEM((rows, part), BF16),
        pltpu.VMEM((rows, part), BF16),
        pltpu.VMEM((rows, part), F32),
        pltpu.SemaphoreType.DMA((7,)),
    ]
    scratch += [pltpu.SemaphoreType.DMA((n_exp - 1,))] * 12
    scratch += [pltpu.SemaphoreType.DMA((n_ten - 1,))] * 2
    scratch += [pltpu.SemaphoreType.DMA((n_exp - 1,))] * 2
    scratch += [pltpu.SemaphoreType.DMA((n_ten - 1,))] * 2
    scratch += [pltpu.SemaphoreType.DMA] * 2
    return pl.pallas_call(
        functools.partial(fused_kernel, n_exp, n_ten),
        out_shape=jax.ShapeDtypeStruct((rows, part), BF16),
        in_specs=[any_spec, vmem, vmem, pl.BlockSpec(memory_space=pltpu.SMEM)] + [any_spec] * 6,
        out_specs=vmem,
        scratch_shapes=scratch,
        compiler_params=pltpu.CompilerParams(
            collective_id=0, has_side_effects=True, vmem_limit_bytes=48 * 1024 * 1024
        ),
    )(*args)


def fits(n_exp, n_ten, tokens, capacity, routed_gate, shared_gate):
    rows, width = tokens.shape
    return (
        n_exp == n_ten
        and n_ten >= 2
        and n_ten & (n_ten - 1) == 0
        and capacity.shape[0] == n_exp
        and routed_gate.shape[0] == 1
        and rows % 32 == 0
        and width % 256 == 0
        and width % (128 * n_exp) == 0
        and shared_gate.shape[1] % 128 == 0
    )


def layer(n_exp, n_ten, *args):
    if fits(n_exp, n_ten, args[0], args[3], args[4], args[7]):
        return fused(n_exp, n_ten, *args)
    return local(*args)


def solution(mesh):
    in_specs = (
        P(("groups", "expert"), None),
        P(("groups", "expert"), None),
        P(("groups", "expert"), None),
        P("groups"),
        P("expert", None, "tensor"),
        P("expert", None, "tensor"),
        P("expert", "tensor", None),
        P("expert", "tensor"),
        P("expert", "tensor"),
        P("expert", "tensor"),
    )
    out_specs = P(("groups", "expert"), "tensor")
    body = functools.partial(layer, mesh.shape["expert"], mesh.shape["tensor"])
    return jax.shard_map(body, mesh=mesh, in_specs=in_specs, out_specs=out_specs, check_vma=False)
```

```python
import functools

import jax
import jax.numpy as jnp
from jax import lax
from jax.experimental import pallas as pl
from jax.experimental.pallas import tpu as pltpu
from jax.sharding import PartitionSpec as P

CAP = 8


def routing_tables(affinity, expert_ids, capacity):
    window = capacity.shape[0]
    tok_rows = expert_ids.shape[0]
    columns = jnp.arange(window, dtype=jnp.int32)
    matches = (expert_ids[:, :, None] == columns[None, None, :]).astype(jnp.float32)
    hit_mask = jnp.sum(matches, axis=1)
    route_weight = (
        2.5
        * jnp.sum(affinity[:, :, None] * matches, axis=1)
        / jnp.sum(affinity, axis=1, keepdims=True)
    )
    earlier = jnp.tril(jnp.ones((tok_rows, tok_rows), jnp.float32), -1)
    slot_index = jnp.dot(earlier, hit_mask, precision=lax.Precision.HIGHEST)
    kept_mask = hit_mask * (slot_index < capacity[None, :].astype(jnp.float32)).astype(jnp.float32)
    levels = jnp.arange(CAP, dtype=jnp.float32)
    placement = kept_mask.T[:, None, :] * (
        slot_index.T[:, None, :] == levels[None, :, None]
    ).astype(jnp.float32)
    return (placement, route_weight)


def local(
    tokens,
    affinity,
    expert_ids,
    capacity,
    routed_gate,
    routed_up,
    routed_down,
    shared_gate,
    shared_up,
    shared_down_t,
):
    gathered_gate, gathered_up, gathered_down = (
        lax.all_gather(shared_gate, "expert", axis=0, tiled=True),
        lax.all_gather(shared_up, "expert", axis=0, tiled=True),
        lax.all_gather(shared_down_t, "expert", axis=0, tiled=True),
    )
    placement, route_weight = routing_tables(affinity, expert_ids, capacity)
    placement_half = placement.astype(jnp.bfloat16)
    outgoing = jnp.einsum(
        "ect,td->ecd", placement_half, tokens, preferred_element_type=jnp.float32
    ).astype(jnp.bfloat16)
    received = lax.all_to_all(outgoing, "expert", split_axis=0, concat_axis=0, tiled=True)
    flat_rows = received.reshape(-1, received.shape[-1])
    gate_rows = jnp.dot(flat_rows, routed_gate[0], preferred_element_type=jnp.float32)
    up_rows = jnp.dot(flat_rows, routed_up[0], preferred_element_type=jnp.float32)
    activated = (jax.nn.silu(gate_rows) * up_rows).astype(jnp.bfloat16)
    partial_out = jnp.dot(activated, routed_down[0], preferred_element_type=jnp.float32)
    partial_out = partial_out.reshape(received.shape[0], received.shape[1], partial_out.shape[-1])
    owner_total = lax.psum_scatter(
        partial_out.astype(jnp.bfloat16), "tensor", scatter_dimension=2, tiled=True
    ).astype(jnp.float32)
    back_rows = lax.all_to_all(
        owner_total.astype(jnp.bfloat16), "expert", split_axis=0, concat_axis=0, tiled=True
    ).astype(owner_total.dtype)
    shared_gate_rows = jnp.dot(tokens, gathered_gate, preferred_element_type=jnp.float32)
    shared_up_rows = jnp.dot(tokens, gathered_up, preferred_element_type=jnp.float32)
    shared_hidden = (jax.nn.silu(shared_gate_rows) * shared_up_rows).astype(jnp.bfloat16)
    shared_out = lax.dot_general(
        shared_hidden, gathered_down, (((1,), (1,)), ((), ())), preferred_element_type=jnp.float32
    )
    weighted = placement * route_weight.T[:, None, :]
    routed_out = jnp.einsum("ect,ecd->td", weighted, back_rows, precision=lax.Precision.HIGHEST)
    summed = lax.psum_scatter(
        shared_out.astype(jnp.bfloat16), "tensor", scatter_dimension=1, tiled=True
    ).astype(jnp.float32)
    mixed_out = summed + routed_out
    return mixed_out.astype(jnp.bfloat16)


SEMAPHORES = 64
VMEM_BYTES = 67043328
RING = 4
MESH = pl.DeviceIdType.MESH
F32 = jnp.float32
BF16 = jnp.bfloat16


def remote(src, dst, send_sem, recv_sem, **device):
    return pltpu.make_async_remote_copy(
        src_ref=src,
        dst_ref=dst,
        send_sem=send_sem,
        recv_sem=recv_sem,
        device_id=device,
        device_id_type=MESH,
    )


def fused_kernel(
    n_exp, n_ten,
    tok_any, aff_ref, ids_ref, cap_ref, rg_any, ru_any, rd_any, sg_any, su_any, sd_any,
    out_ref,
    tok, wgu, wdn, rgw, ruw, rdw, xall, xrel, gown, gpart, gsend, gin, hall, weights,
    rout, rin, ys, yin, yb, back, acc, osend, oin, rsend, rfin, routed,
    lsem, ssem, rsem,
):
    e, t = lax.axis_index("expert"), lax.axis_index("tensor")
    core = lax.rem(t, 2)
    partner = t + 1 - 2 * core
    rows, width = tok.shape
    cols = width // n_exp
    half = rows // 2
    half_width = width // 2
    hidden = hall.shape[2]
    others = range(1, n_exp)
    started = []

    def link(src, dst, **device):
        at = len(started)
        copy = remote(src, dst, ssem.at[at], rsem.at[at], **device)
        copy.start()
        started.append(copy)
        return copy

    def up(k):
        return lax.rem(e + k + n_exp, n_exp)

    def span(index, size, unit=128):
        return pl.ds(pl.multiple_of(index * size, unit), size)

    right, left, opposite = up(1), up(-1), up(n_exp // 2)

    loads = [
        pltpu.make_async_copy(tok_any, tok, lsem.at[0]),
        pltpu.make_async_copy(sg_any, wgu.at[:, pl.ds(0, hidden)], lsem.at[1]),
        pltpu.make_async_copy(su_any, wgu.at[:, pl.ds(hidden, hidden)], lsem.at[2]),
        pltpu.make_async_copy(rg_any.at[0], rgw, lsem.at[3]),
        pltpu.make_async_copy(ru_any.at[0], ruw, lsem.at[4]),
        pltpu.make_async_copy(rd_any.at[0], rdw, lsem.at[5]),
        pltpu.make_async_copy(sd_any, wdn, lsem.at[6]),
    ]
    for load in loads:
        load.start()

    barrier = pltpu.get_barrier_semaphore()
    for k in others:
        pl.semaphore_signal(barrier, inc=1, device_id={"expert": up(k)}, device_id_type=MESH)
    for k in range(1, n_ten):
        pl.semaphore_signal(
            barrier, inc=1, device_id={"tensor": lax.rem(t + k, n_ten)}, device_id_type=MESH
        )

    @pl.when(e != t)
    def _():
        pl.semaphore_signal(
            barrier, inc=1, device_id={"expert": t, "tensor": e}, device_id_type=MESH
        )

    pl.semaphore_wait(barrier, n_exp + n_ten - 2 + (e != t).astype(jnp.int32))

    mine = span(core, half, 16)
    large = (cols // 128 + 1) // 2 * 128
    ahead, behind = up(1 - 2 * core), up(2 * core - 1)
    x_copy = {}
    for name, to in (("left", right), ("right", left)):
        x_copy[name] = link(
            tok_any.at[mine, span(to, cols)], xall.at[e, mine, :], expert=to
        )
    first = pl.multiple_of(opposite * cols, 128)
    x_large = link(
        tok_any.at[mine, pl.ds(first, large)], xrel.at[:, pl.ds(0, large)], expert=ahead
    )
    x_small = link(
        tok_any.at[mine, pl.ds(first + large, cols - large)],
        xrel.at[:, pl.ds(large, cols - large)],
        expert=behind,
    )

    lanes = n_exp * CAP
    line = lax.broadcasted_iota(jnp.int32, (lanes, rows), 0)
    expert_of, level = line // CAP, lax.rem(line, CAP)
    ids, aff = ids_ref[...], aff_ref[...]
    hit = jnp.zeros((lanes, rows), F32)
    chosen = jnp.zeros((lanes, rows), F32)
    for k in range(ids.shape[0]):
        match = (ids[k : k + 1, :] == expert_of).astype(F32)
        hit += match
        chosen += match * aff[k : k + 1, :]
    share = 2.5 * chosen / jnp.sum(aff, axis=0, keepdims=True)
    earlier = (
        lax.broadcasted_iota(jnp.int32, (rows, rows), 0)
        < lax.broadcasted_iota(jnp.int32, (rows, rows), 1)
    ).astype(BF16)
    slot = jnp.dot(hit.astype(BF16), earlier, preferred_element_type=F32)
    limit = jnp.zeros((lanes, rows), jnp.int32)
    for k in range(n_exp):
        limit = jnp.where(expert_of == k, cap_ref[k], limit)
    placed = (
        hit * (slot < limit.astype(F32)).astype(F32) * (slot == level.astype(F32)).astype(F32)
    )
    weights[...] = jnp.transpose(placed * share)
    loads[0].wait()
    chosen_rows = jnp.dot(placed.astype(BF16), tok[...], preferred_element_type=F32)
    for k in range(n_exp):
        rout[k] = chosen_rows[k * CAP : (k + 1) * CAP].astype(BF16)
    rin[e] = rout[e]

    x_pass = {}
    for name, index in (("left", left), ("right", right)):
        x_copy[name].wait_recv()
        x_pass[name] = link(
            xall.at[index, mine, :], xall.at[index, mine, :], tensor=partner
        )
    x_large.wait_recv()
    whole_large = xall.at[behind, mine, pl.ds(0, large)]
    x_large = link(xrel.at[:, pl.ds(0, large)], whole_large, expert=ahead)
    x_small.wait_recv()
    whole_small = xall.at[ahead, mine, pl.ds(large, cols - large)]
    x_small = link(xrel.at[:, pl.ds(large, cols - large)], whole_small, expert=behind)
    loads[1].wait()
    loads[2].wait()

    lower, upper = pl.ds(0, hidden), pl.ds(hidden, hidden)

    def project(index):
        return jnp.dot(xall[index], wgu[...], preferred_element_type=F32)

    x_pass["left"].wait_recv()
    found = project(left)
    gsend[0] = found[:, :hidden].astype(BF16)
    gpart[0] = found[:, hidden:]
    g_left = link(gsend.at[0], gin.at[0], expert=left)
    x_pass["right"].wait_recv()
    found = project(right)
    gsend[1] = found[:, hidden:].astype(BF16)
    gpart[1] = found[:, :hidden]
    g_right = link(gsend.at[1], gin.at[1], expert=right)

    side = span(core, half_width)
    b_copy = {}
    for k in others:
        b_copy[k] = link(rout.at[up(k), :, side], rin.at[e, :, side], expert=up(k))

    x_large.wait_recv()
    x_small.wait_recv()
    x_far = link(
        xall.at[opposite, mine, :], xall.at[opposite, mine, :], tensor=partner
    )
    x_far.wait_recv()
    found = project(opposite)
    gsend[2] = found[:, :hidden].astype(BF16)
    g_low = link(gsend.at[2], gin.at[2], expert=right)
    gsend[3] = found[:, hidden:].astype(BF16)
    g_high = link(gsend.at[3], gin.at[3], expert=left)
    gown[...] = jnp.dot(tok[:, span(e, cols)], wgu[...], preferred_element_type=F32)
    b_pass = {}
    for k in others:
        b_copy[k].wait_recv()
        b_pass[k] = link(
            rin.at[up(-k), :, side], rin.at[up(-k), :, side], tensor=partner
        )
    g_low.wait_recv()
    gsend[4] = (gpart[1] + gin[2].astype(F32)).astype(BF16)
    g_low = link(gsend.at[4], gin.at[4], expert=right)
    g_high.wait_recv()
    gsend[5] = (gpart[0] + gin[3].astype(F32)).astype(BF16)
    g_high = link(gsend.at[5], gin.at[5], expert=left)

    for load in loads[3:]:
        load.wait()
    for k in others:
        b_pass[k].wait_recv()
    flat = jnp.concatenate([rin[k].astype(F32) for k in range(n_exp)], axis=0).astype(BF16)
    gate = jnp.dot(flat, rgw[...], preferred_element_type=F32)
    above = jnp.dot(flat, ruw[...], preferred_element_type=F32)
    act = (gate * (1.0 / (1.0 + jnp.exp(-gate))) * above).astype(BF16)
    ys[...] = jnp.dot(act, rdw[...], preferred_element_type=F32).astype(BF16)
    y_copy = {}
    part = width // n_ten
    for k in range(1, n_ten):
        to = lax.rem(t + k, n_ten)
        y_copy[k] = link(ys.at[:, span(to, part)], yin.at[k - 1], tensor=to)

    g_left.wait_recv()
    g_right.wait_recv()
    g_low.wait_recv()
    g_high.wait_recv()
    gate = gown[:, :hidden] + gin[0].astype(F32) + gin[4].astype(F32)
    above = gown[:, hidden:] + gin[1].astype(F32) + gin[5].astype(F32)
    hall[e] = (gate * (1.0 / (1.0 + jnp.exp(-gate))) * above).astype(BF16)
    near, far = pl.ds(0, hidden // 2), pl.ds(hidden // 2, hidden // 2)
    from_left = link(hall.at[e, :, near], hall.at[e, :, near], expert=right)
    from_right = link(hall.at[e, :, far], hall.at[e, :, far], expert=left)
    rest_left = link(hall.at[e, :, far], hall.at[e, :, far], expert=right)
    rest_right = link(hall.at[e, :, near], hall.at[e, :, near], expert=left)

    total = ys[:, span(t, part)].astype(F32)
    for k in range(1, n_ten):
        y_copy[k].wait_recv()
        total = total + yin[k - 1].astype(F32)
    for k in range(n_exp):
        yb[k] = total[k * CAP : (k + 1) * CAP].astype(BF16)
    back[e] = yb[e]

    from_left.wait_recv()
    from_left = link(hall.at[left, :, near], hall.at[left, :, near], expert=right)
    from_right.wait_recv()
    from_right = link(hall.at[right, :, far], hall.at[right, :, far], expert=left)
    k_copy = {}
    for k in others:
        k_copy[k] = link(yb.at[up(k)], back.at[e], expert=up(k))

    def product(index):
        return lax.dot_general(
            hall[index], wdn[...], (((1,), (1,)), ((), ())), preferred_element_type=F32
        )

    acc[e] = product(e)
    rest_left.wait_recv()
    acc[left] = product(left)
    rest_right.wait_recv()
    acc[right] = product(right)
    from_left.wait_recv()
    from_right.wait_recv()
    acc[opposite] = product(opposite)

    bits = n_ten.bit_length() - 1
    place = 0
    for s in range(bits):
        bit = lax.rem(t // (1 << s), 2)
        low = lax.rem(t, 1 << s)
        peer = t + (1 - 2 * bit) * (1 << s)
        count = n_ten >> (s + 1)
        copies = []
        for i in range(count):
            sent = (2 * i + 1 - bit) * (1 << s) + low
            osend[place + i] = acc[sent].astype(BF16)
            copies.append(link(osend.at[place + i], oin.at[place + i], tensor=peer))
        for i in range(count):
            kept = (2 * i + bit) * (1 << s) + low
            copies[i].wait_recv()
            acc[kept] = acc[kept] + oin[place + i].astype(F32)
        place += count
    at = len(started)
    final = remote(rsend, rfin, ssem.at[at], rsem.at[at], expert=t, tensor=e)

    @pl.when(e != t)
    def _():
        rsend[...] = acc[t].astype(BF16)
        final.start()

    @pl.when(e == t)
    def _():
        rfin[...] = acc[t].astype(BF16)

    for k in others:
        k_copy[k].wait_recv()
    rows_back = jnp.concatenate([back[k].astype(F32) for k in range(n_exp)], axis=0)
    routed[...] = jnp.dot(
        weights[...], rows_back, preferred_element_type=F32, precision=lax.Precision.HIGHEST
    )

    @pl.when(e != t)
    def _():
        final.wait()

    out_ref[...] = (rfin[...].astype(F32) + routed[...]).astype(BF16)
    for copy in started:
        copy.wait_send()


def fused(n_exp, n_ten, *args):
    tokens, affinity, expert_ids, capacity, rg, ru, rd, sg, su, sd = args
    rows, width = tokens.shape
    hidden = sg.shape[1]
    cols, part = width // n_exp, width // n_ten
    any_spec = pl.BlockSpec(memory_space=pl.ANY)
    vmem = pl.BlockSpec(memory_space=pltpu.VMEM)
    scratch = [
        pltpu.VMEM((rows, width), BF16),
        pltpu.VMEM((cols, 2 * hidden), BF16),
        pltpu.VMEM((cols, hidden), BF16),
        pltpu.VMEM(rg.shape[1:], BF16),
        pltpu.VMEM(ru.shape[1:], BF16),
        pltpu.VMEM(rd.shape[1:], BF16),
        pltpu.VMEM((n_exp, rows, cols), BF16),
        pltpu.VMEM((rows // 2, cols), BF16),
        pltpu.VMEM((rows, 2 * hidden), F32),
        pltpu.VMEM((2, rows, hidden), F32),
        pltpu.VMEM((6, rows, hidden), BF16),
        pltpu.VMEM((6, rows, hidden), BF16),
        pltpu.VMEM((n_exp, rows, hidden), BF16),
        pltpu.VMEM((rows, n_exp * CAP), F32),
        pltpu.VMEM((n_exp, CAP, width), BF16),
        pltpu.VMEM((n_exp, CAP, width), BF16),
        pltpu.VMEM((n_exp * CAP, width), BF16),
        pltpu.VMEM((n_ten - 1, n_exp * CAP, part), BF16),
        pltpu.VMEM((n_exp, CAP, part), BF16),
        pltpu.VMEM((n_exp, CAP, part), BF16),
        pltpu.VMEM((n_ten, rows, part), F32),
        pltpu.VMEM((n_ten - 1, rows, part), BF16),
        pltpu.VMEM((n_ten - 1, rows, part), BF16),
        pltpu.VMEM((rows, part), BF16),
        pltpu.VMEM((rows, part), BF16),
        pltpu.VMEM((rows, part), F32),
        pltpu.SemaphoreType.DMA((7,)),
        pltpu.SemaphoreType.DMA((SEMAPHORES,)),
        pltpu.SemaphoreType.DMA((SEMAPHORES,)),
    ]
    return pl.pallas_call(
        functools.partial(fused_kernel, n_exp, n_ten),
        out_shape=jax.ShapeDtypeStruct((rows, part), BF16),
        in_specs=[any_spec, vmem, vmem, pl.BlockSpec(memory_space=pltpu.SMEM)] + [any_spec] * 6,
        out_specs=vmem,
        scratch_shapes=scratch,
        compiler_params=pltpu.CompilerParams(
            collective_id=0, has_side_effects=True, vmem_limit_bytes=VMEM_BYTES
        ),
    )(tokens, affinity.T, expert_ids.T, *args[3:])


def fits(n_exp, n_ten, tokens, capacity, routed_gate, shared_gate):
    rows, width = tokens.shape
    return (
        n_exp == RING
        and n_ten == n_exp
        and capacity.shape[0] == n_exp
        and routed_gate.shape[0] == 1
        and rows % 32 == 0
        and width % 256 == 0
        and width // n_exp >= 256
        and width % (128 * n_exp) == 0
        and shared_gate.shape[1] % 256 == 0
    )


def layer(n_exp, n_ten, *args):
    if fits(n_exp, n_ten, args[0], args[3], args[4], args[7]):
        return fused(n_exp, n_ten, *args)
    return local(*args)


def solution(mesh):
    in_specs = (
        P(("groups", "expert"), None),
        P(("groups", "expert"), None),
        P(("groups", "expert"), None),
        P("groups"),
        P("expert", None, "tensor"),
        P("expert", None, "tensor"),
        P("expert", "tensor", None),
        P("expert", "tensor"),
        P("expert", "tensor"),
        P("expert", "tensor"),
    )
    out_specs = P(("groups", "expert"), "tensor")
    body = functools.partial(layer, mesh.shape["expert"], mesh.shape["tensor"])
    return jax.shard_map(body, mesh=mesh, in_specs=in_specs, out_specs=out_specs, check_vma=False)
```

```python
import functools

import jax
import jax.numpy as jnp
from jax import lax
from jax.experimental import pallas as pl
from jax.experimental.pallas import tpu as pltpu
from jax.sharding import PartitionSpec as P

CAP = 8


def routing_tables(affinity, expert_ids, capacity):
    window = capacity.shape[0]
    tok_rows = expert_ids.shape[0]
    columns = jnp.arange(window, dtype=jnp.int32)
    matches = (expert_ids[:, :, None] == columns[None, None, :]).astype(jnp.float32)
    hit_mask = jnp.sum(matches, axis=1)
    route_weight = (
        2.5
        * jnp.sum(affinity[:, :, None] * matches, axis=1)
        / jnp.sum(affinity, axis=1, keepdims=True)
    )
    earlier = jnp.tril(jnp.ones((tok_rows, tok_rows), jnp.float32), -1)
    slot_index = jnp.dot(earlier, hit_mask, precision=lax.Precision.HIGHEST)
    kept_mask = hit_mask * (slot_index < capacity[None, :].astype(jnp.float32)).astype(jnp.float32)
    levels = jnp.arange(CAP, dtype=jnp.float32)
    placement = kept_mask.T[:, None, :] * (
        slot_index.T[:, None, :] == levels[None, :, None]
    ).astype(jnp.float32)
    return (placement, route_weight)


def local(
    tokens,
    affinity,
    expert_ids,
    capacity,
    routed_gate,
    routed_up,
    routed_down,
    shared_gate,
    shared_up,
    shared_down_t,
):
    gathered_gate, gathered_up, gathered_down = (
        lax.all_gather(shared_gate, "expert", axis=0, tiled=True),
        lax.all_gather(shared_up, "expert", axis=0, tiled=True),
        lax.all_gather(shared_down_t, "expert", axis=0, tiled=True),
    )
    placement, route_weight = routing_tables(affinity, expert_ids, capacity)
    placement_half = placement.astype(jnp.bfloat16)
    outgoing = jnp.einsum(
        "ect,td->ecd", placement_half, tokens, preferred_element_type=jnp.float32
    ).astype(jnp.bfloat16)
    received = lax.all_to_all(outgoing, "expert", split_axis=0, concat_axis=0, tiled=True)
    flat_rows = received.reshape(-1, received.shape[-1])
    gate_rows = jnp.dot(flat_rows, routed_gate[0], preferred_element_type=jnp.float32)
    up_rows = jnp.dot(flat_rows, routed_up[0], preferred_element_type=jnp.float32)
    activated = (jax.nn.silu(gate_rows) * up_rows).astype(jnp.bfloat16)
    partial_out = jnp.dot(activated, routed_down[0], preferred_element_type=jnp.float32)
    partial_out = partial_out.reshape(received.shape[0], received.shape[1], partial_out.shape[-1])
    owner_total = lax.psum_scatter(
        partial_out.astype(jnp.bfloat16), "tensor", scatter_dimension=2, tiled=True
    ).astype(jnp.float32)
    back_rows = lax.all_to_all(
        owner_total.astype(jnp.bfloat16), "expert", split_axis=0, concat_axis=0, tiled=True
    ).astype(owner_total.dtype)
    shared_gate_rows = jnp.dot(tokens, gathered_gate, preferred_element_type=jnp.float32)
    shared_up_rows = jnp.dot(tokens, gathered_up, preferred_element_type=jnp.float32)
    shared_hidden = (jax.nn.silu(shared_gate_rows) * shared_up_rows).astype(jnp.bfloat16)
    shared_out = lax.dot_general(
        shared_hidden, gathered_down, (((1,), (1,)), ((), ())), preferred_element_type=jnp.float32
    )
    weighted = placement * route_weight.T[:, None, :]
    routed_out = jnp.einsum("ect,ecd->td", weighted, back_rows, precision=lax.Precision.HIGHEST)
    summed = lax.psum_scatter(
        shared_out.astype(jnp.bfloat16), "tensor", scatter_dimension=1, tiled=True
    ).astype(jnp.float32)
    mixed_out = summed + routed_out
    return mixed_out.astype(jnp.bfloat16)


SEMAPHORES = 64
VMEM_BYTES = 67043328
RING = 4
MESH = pl.DeviceIdType.MESH
F32 = jnp.float32
BF16 = jnp.bfloat16


def remote(src, dst, send_sem, recv_sem, **device):
    return pltpu.make_async_remote_copy(
        src_ref=src,
        dst_ref=dst,
        send_sem=send_sem,
        recv_sem=recv_sem,
        device_id=device,
        device_id_type=MESH,
    )


def fused_kernel(
    n_exp, n_ten,
    tok_any, aff_ref, ids_ref, cap_ref, rg_any, ru_any, rd_any, sg_any, su_any, sd_any,
    out_ref,
    tok, wgu, wdn, rgw, ruw, rdw, xall, xrel, gown, gpart, gsend, gin, hall, weights,
    rout, rin, ys, yin, yb, back, acc, osend, oin, xsend, xin, fsend, rfin, routed,
    lsem, ssem, rsem, cs, cr, xs, xr, fs, fr,
):
    e, t = lax.axis_index("expert"), lax.axis_index("tensor")
    core = lax.rem(t, 2)
    partner = t + 1 - 2 * core
    rows, width = tok.shape
    cols = width // n_exp
    half = rows // 2
    half_width = width // 2
    hidden = hall.shape[2]
    others = range(1, n_exp)
    started = []

    def link(src, dst, **device):
        at = len(started)
        copy = remote(src, dst, ssem.at[at], rsem.at[at], **device)
        copy.start()
        started.append(copy)
        return copy

    def up(k):
        return lax.rem(e + k + n_exp, n_exp)

    def span(index, size, unit=128):
        return pl.ds(pl.multiple_of(index * size, unit), size)

    right, left, opposite = up(1), up(-1), up(n_exp // 2)

    loads = [
        pltpu.make_async_copy(tok_any, tok, lsem.at[0]),
        pltpu.make_async_copy(sg_any, wgu.at[:, pl.ds(0, hidden)], lsem.at[1]),
        pltpu.make_async_copy(su_any, wgu.at[:, pl.ds(hidden, hidden)], lsem.at[2]),
        pltpu.make_async_copy(rg_any.at[0], rgw, lsem.at[3]),
        pltpu.make_async_copy(ru_any.at[0], ruw, lsem.at[4]),
        pltpu.make_async_copy(rd_any.at[0], rdw, lsem.at[5]),
        pltpu.make_async_copy(sd_any, wdn, lsem.at[6]),
    ]
    loads[0].start()

    barrier = pltpu.get_barrier_semaphore()
    for i in range(n_exp):
        for j in range(n_ten):
            if i or j:
                pl.semaphore_signal(
                    barrier,
                    inc=1,
                    device_id={"expert": up(i), "tensor": lax.rem(t + j, n_ten)},
                    device_id_type=MESH,
                )
    pl.semaphore_wait(barrier, n_exp * n_ten - 1)

    mine = span(core, half, 16)
    large = (cols // 128 + 1) // 2 * 128
    ahead, behind = up(1 - 2 * core), up(2 * core - 1)
    x_copy = {}
    for name, to in (("left", right), ("right", left)):
        x_copy[name] = link(
            tok_any.at[mine, span(to, cols)], xall.at[e, mine, :], expert=to
        )
    first = pl.multiple_of(opposite * cols, 128)
    x_large = link(
        tok_any.at[mine, pl.ds(first, large)], xrel.at[:, pl.ds(0, large)], expert=ahead
    )
    x_small = link(
        tok_any.at[mine, pl.ds(first + large, cols - large)],
        xrel.at[:, pl.ds(large, cols - large)],
        expert=behind,
    )

    for load in loads[1:]:
        load.start()

    lanes = n_exp * CAP
    line = lax.broadcasted_iota(jnp.int32, (lanes, rows), 0)
    expert_of, level = line // CAP, lax.rem(line, CAP)
    ids, aff = ids_ref[...], aff_ref[...]
    hit = jnp.zeros((lanes, rows), F32)
    chosen = jnp.zeros((lanes, rows), F32)
    for k in range(ids.shape[0]):
        match = (ids[k : k + 1, :] == expert_of).astype(F32)
        hit += match
        chosen += match * aff[k : k + 1, :]
    share = 2.5 * chosen / jnp.sum(aff, axis=0, keepdims=True)
    earlier = (
        lax.broadcasted_iota(jnp.int32, (rows, rows), 0)
        < lax.broadcasted_iota(jnp.int32, (rows, rows), 1)
    ).astype(BF16)
    slot = jnp.dot(hit.astype(BF16), earlier, preferred_element_type=F32)
    limit = jnp.zeros((lanes, rows), jnp.int32)
    for k in range(n_exp):
        limit = jnp.where(expert_of == k, cap_ref[k], limit)
    placed = (
        hit * (slot < limit.astype(F32)).astype(F32) * (slot == level.astype(F32)).astype(F32)
    )
    weights[...] = jnp.transpose(placed * share)
    loads[0].wait()
    chosen_rows = jnp.dot(placed.astype(BF16), tok[...], preferred_element_type=F32)
    for k in range(n_exp):
        rout[k] = chosen_rows[k * CAP : (k + 1) * CAP].astype(BF16)
    rin[e] = rout[e]

    x_pass = {}
    for name, index in (("left", left), ("right", right)):
        x_copy[name].wait_recv()
        x_pass[name] = link(
            xall.at[index, mine, :], xall.at[index, mine, :], tensor=partner
        )
    x_large.wait_recv()
    whole_large = xall.at[behind, mine, pl.ds(0, large)]
    x_large = link(xrel.at[:, pl.ds(0, large)], whole_large, expert=ahead)
    x_small.wait_recv()
    whole_small = xall.at[ahead, mine, pl.ds(large, cols - large)]
    x_small = link(xrel.at[:, pl.ds(large, cols - large)], whole_small, expert=behind)
    loads[1].wait()
    loads[2].wait()

    lower, upper = pl.ds(0, hidden), pl.ds(hidden, hidden)

    def project(index):
        return jnp.dot(xall[index], wgu[...], preferred_element_type=F32)

    x_pass["left"].wait_recv()
    found = project(left)
    gsend[0] = found[:, :hidden].astype(BF16)
    gpart[0] = found[:, hidden:]
    g_left = link(gsend.at[0], gin.at[0], expert=left)
    x_pass["right"].wait_recv()
    found = project(right)
    gsend[1] = found[:, hidden:].astype(BF16)
    gpart[1] = found[:, :hidden]
    g_right = link(gsend.at[1], gin.at[1], expert=right)

    side = span(core, half_width)
    b_copy = {}
    for k in others:
        b_copy[k] = link(rout.at[up(k), :, side], rin.at[e, :, side], expert=up(k))

    x_large.wait_recv()
    x_small.wait_recv()
    x_far = link(
        xall.at[opposite, mine, :], xall.at[opposite, mine, :], tensor=partner
    )
    x_far.wait_recv()
    found = project(opposite)
    gsend[2] = found[:, :hidden].astype(BF16)
    g_low = link(gsend.at[2], gin.at[2], expert=right)
    gsend[3] = found[:, hidden:].astype(BF16)
    g_high = link(gsend.at[3], gin.at[3], expert=left)
    gown[...] = jnp.dot(tok[:, span(e, cols)], wgu[...], preferred_element_type=F32)
    b_pass = {}
    for k in others:
        b_copy[k].wait_recv()
        b_pass[k] = link(
            rin.at[up(-k), :, side], rin.at[up(-k), :, side], tensor=partner
        )
    g_low.wait_recv()
    gsend[4] = (gpart[1] + gin[2].astype(F32)).astype(BF16)
    g_low = link(gsend.at[4], gin.at[4], expert=right)
    g_high.wait_recv()
    gsend[5] = (gpart[0] + gin[3].astype(F32)).astype(BF16)
    g_high = link(gsend.at[5], gin.at[5], expert=left)

    for load in loads[3:]:
        load.wait()
    for k in others:
        b_pass[k].wait_recv()
    flat = jnp.concatenate([rin[k].astype(F32) for k in range(n_exp)], axis=0).astype(BF16)
    gate = jnp.dot(flat, rgw[...], preferred_element_type=F32)
    above = jnp.dot(flat, ruw[...], preferred_element_type=F32)
    act = (gate * (1.0 / (1.0 + jnp.exp(-gate))) * above).astype(BF16)
    ys[...] = jnp.dot(act, rdw[...], preferred_element_type=F32).astype(BF16)
    y_copy = {}
    part = width // n_ten
    for k in range(1, n_ten):
        to = lax.rem(t + k, n_ten)
        y_copy[k] = link(ys.at[:, span(to, part)], yin.at[k - 1], tensor=to)

    g_left.wait_recv()
    g_right.wait_recv()
    g_low.wait_recv()
    g_high.wait_recv()
    gate = gown[:, :hidden] + gin[0].astype(F32) + gin[4].astype(F32)
    above = gown[:, hidden:] + gin[1].astype(F32) + gin[5].astype(F32)
    hall[e] = (gate * (1.0 / (1.0 + jnp.exp(-gate))) * above).astype(BF16)
    near, far = pl.ds(0, hidden // 2), pl.ds(hidden // 2, hidden // 2)
    from_left = link(hall.at[e, :, near], hall.at[e, :, near], expert=right)
    from_right = link(hall.at[e, :, far], hall.at[e, :, far], expert=left)
    rest_left = link(hall.at[e, :, far], hall.at[e, :, far], expert=right)
    rest_right = link(hall.at[e, :, near], hall.at[e, :, near], expert=left)

    total = ys[:, span(t, part)].astype(F32)
    for k in range(1, n_ten):
        y_copy[k].wait_recv()
        total = total + yin[k - 1].astype(F32)
    for k in range(n_exp):
        yb[k] = total[k * CAP : (k + 1) * CAP].astype(BF16)
    back[e] = yb[e]

    from_left.wait_recv()
    from_left = link(hall.at[left, :, near], hall.at[left, :, near], expert=right)
    from_right.wait_recv()
    from_right = link(hall.at[right, :, far], hall.at[right, :, far], expert=left)
    k_copy = {}
    for k in others:
        k_copy[k] = link(yb.at[up(k)], back.at[e], expert=up(k))

    def product(index):
        return lax.dot_general(
            hall[index], wdn[...], (((1,), (1,)), ((), ())), preferred_element_type=F32
        )

    x_bit = t // 2
    x_peer = lax.rem(t + 2, n_ten)
    keep_half, give_half = span(x_bit, half, 16), span(1 - x_bit, half, 16)
    blocks = [e, left, right, opposite]
    arrivals = [[], [rest_left], [rest_right], [from_left, from_right]]

    def core_copy(j):
        return remote(osend.at[j], oin.at[j], cs.at[j], cr.at[j], tensor=partner)

    def x_copy_of(j):
        return remote(xsend.at[j], xin.at[j], xs.at[j], xr.at[j], tensor=x_peer)

    def last_copy(j):
        return remote(
            fsend.at[j], rfin.at[keep_half, :], fs.at[j], fr.at[x_bit],
            expert=blocks[j], tensor=e,
        )

    def compute(j):
        for copy in arrivals[j]:
            copy.wait_recv()
        return product(blocks[j])

    def give(j):
        osend[j] = compute(j).astype(BF16)
        core_copy(j).start()

    def take(j):
        acc[j] = compute(j)
        core_copy(j).wait_recv()
        xsend[j] = (acc[j, give_half, :] + oin[j, give_half, :].astype(F32)).astype(BF16)
        x_copy_of(j).start()

    def finish(j):
        both = acc[j, keep_half, :] + oin[j, keep_half, :].astype(F32)
        x_copy_of(j).wait_recv()
        value = (both + xin[j].astype(F32)).astype(BF16)
        if j:
            fsend[j] = value
            last_copy(j).start()
        else:

            @pl.when(e == t)
            def _():
                rfin[keep_half, :] = value

            @pl.when(e != t)
            def _():
                fsend[j] = value
                last_copy(j).start()

    def settle(kept, given):
        for j in given:
            core_copy(j).wait_send()
        for j in kept:
            x_copy_of(j).wait_send()
            if j:
                last_copy(j).wait_send()
            else:

                @pl.when(e != t)
                def _():
                    last_copy(j).wait_send()

    even = lax.rem(e + core, 2) == 0

    @pl.when(even)
    def _():
        take(0)
        give(1)
        give(2)
        finish(0)
        take(3)
        finish(3)
        settle((0, 3), (1, 2))

    @pl.when(jnp.logical_not(even))
    def _():
        give(0)
        take(1)
        take(2)
        finish(1)
        finish(2)
        give(3)
        settle((1, 2), (0, 3))

    for k in others:
        k_copy[k].wait_recv()
    rows_back = jnp.concatenate([back[k].astype(F32) for k in range(n_exp)], axis=0)
    routed[...] = jnp.dot(
        weights[...], rows_back, preferred_element_type=F32, precision=lax.Precision.HIGHEST
    )

    for h in range(2):

        @pl.when(jnp.logical_or(e != t, x_bit != h))
        def _():
            remote(
                fsend.at[0], rfin.at[pl.ds(h * half, half), :], fs.at[0], fr.at[h],
                expert=t, tensor=e,
            ).wait_recv()

    out_ref[...] = (rfin[...].astype(F32) + routed[...]).astype(BF16)
    for copy in started:
        copy.wait_send()


def fused(n_exp, n_ten, *args):
    tokens, affinity, expert_ids, capacity, rg, ru, rd, sg, su, sd = args
    rows, width = tokens.shape
    hidden = sg.shape[1]
    cols, part = width // n_exp, width // n_ten
    any_spec = pl.BlockSpec(memory_space=pl.ANY)
    vmem = pl.BlockSpec(memory_space=pltpu.VMEM)
    scratch = [
        pltpu.VMEM((rows, width), BF16),
        pltpu.VMEM((cols, 2 * hidden), BF16),
        pltpu.VMEM((cols, hidden), BF16),
        pltpu.VMEM(rg.shape[1:], BF16),
        pltpu.VMEM(ru.shape[1:], BF16),
        pltpu.VMEM(rd.shape[1:], BF16),
        pltpu.VMEM((n_exp, rows, cols), BF16),
        pltpu.VMEM((rows // 2, cols), BF16),
        pltpu.VMEM((rows, 2 * hidden), F32),
        pltpu.VMEM((2, rows, hidden), F32),
        pltpu.VMEM((6, rows, hidden), BF16),
        pltpu.VMEM((6, rows, hidden), BF16),
        pltpu.VMEM((n_exp, rows, hidden), BF16),
        pltpu.VMEM((rows, n_exp * CAP), F32),
        pltpu.VMEM((n_exp, CAP, width), BF16),
        pltpu.VMEM((n_exp, CAP, width), BF16),
        pltpu.VMEM((n_exp * CAP, width), BF16),
        pltpu.VMEM((n_ten - 1, n_exp * CAP, part), BF16),
        pltpu.VMEM((n_exp, CAP, part), BF16),
        pltpu.VMEM((n_exp, CAP, part), BF16),
        pltpu.VMEM((n_exp, rows, part), F32),
        pltpu.VMEM((n_exp, rows, part), BF16),
        pltpu.VMEM((n_exp, rows, part), BF16),
        pltpu.VMEM((n_exp, rows // 2, part), BF16),
        pltpu.VMEM((n_exp, rows // 2, part), BF16),
        pltpu.VMEM((n_exp, rows // 2, part), BF16),
        pltpu.VMEM((rows, part), BF16),
        pltpu.VMEM((rows, part), F32),
        pltpu.SemaphoreType.DMA((7,)),
        pltpu.SemaphoreType.DMA((SEMAPHORES,)),
        pltpu.SemaphoreType.DMA((SEMAPHORES,)),
    ]
    scratch += [pltpu.SemaphoreType.DMA((n_exp,))] * 5 + [pltpu.SemaphoreType.DMA((2,))]
    return pl.pallas_call(
        functools.partial(fused_kernel, n_exp, n_ten),
        out_shape=jax.ShapeDtypeStruct((rows, part), BF16),
        in_specs=[any_spec, vmem, vmem, pl.BlockSpec(memory_space=pltpu.SMEM)] + [any_spec] * 6,
        out_specs=vmem,
        scratch_shapes=scratch,
        compiler_params=pltpu.CompilerParams(
            collective_id=0, has_side_effects=True, vmem_limit_bytes=VMEM_BYTES
        ),
    )(tokens, affinity.T, expert_ids.T, *args[3:])


def fits(n_exp, n_ten, tokens, capacity, routed_gate, shared_gate):
    rows, width = tokens.shape
    return (
        n_exp == RING
        and n_ten == n_exp
        and capacity.shape[0] == n_exp
        and routed_gate.shape[0] == 1
        and rows % 32 == 0
        and width % 256 == 0
        and width // n_exp >= 256
        and width % (128 * n_exp) == 0
        and shared_gate.shape[1] % 256 == 0
    )


def layer(n_exp, n_ten, *args):
    if fits(n_exp, n_ten, args[0], args[3], args[4], args[7]):
        return fused(n_exp, n_ten, *args)
    return local(*args)


def solution(mesh):
    in_specs = (
        P(("groups", "expert"), None),
        P(("groups", "expert"), None),
        P(("groups", "expert"), None),
        P("groups"),
        P("expert", None, "tensor"),
        P("expert", None, "tensor"),
        P("expert", "tensor", None),
        P("expert", "tensor"),
        P("expert", "tensor"),
        P("expert", "tensor"),
    )
    out_specs = P(("groups", "expert"), "tensor")
    body = functools.partial(layer, mesh.shape["expert"], mesh.shape["tensor"])
    return jax.shard_map(body, mesh=mesh, in_specs=in_specs, out_specs=out_specs, check_vma=False)
```

```python
import functools

import jax
import jax.numpy as jnp
from jax import lax
from jax.experimental import pallas as pl
from jax.experimental.pallas import tpu as pltpu
from jax.sharding import PartitionSpec as P

CAP = 8


def routing_tables(affinity, expert_ids, capacity):
    window = capacity.shape[0]
    tok_rows = expert_ids.shape[0]
    columns = jnp.arange(window, dtype=jnp.int32)
    matches = (expert_ids[:, :, None] == columns[None, None, :]).astype(jnp.float32)
    hit_mask = jnp.sum(matches, axis=1)
    route_weight = (
        2.5
        * jnp.sum(affinity[:, :, None] * matches, axis=1)
        / jnp.sum(affinity, axis=1, keepdims=True)
    )
    earlier = jnp.tril(jnp.ones((tok_rows, tok_rows), jnp.float32), -1)
    slot_index = jnp.dot(earlier, hit_mask, precision=lax.Precision.HIGHEST)
    kept_mask = hit_mask * (slot_index < capacity[None, :].astype(jnp.float32)).astype(jnp.float32)
    levels = jnp.arange(CAP, dtype=jnp.float32)
    placement = kept_mask.T[:, None, :] * (
        slot_index.T[:, None, :] == levels[None, :, None]
    ).astype(jnp.float32)
    return (placement, route_weight)


def local(
    tokens,
    affinity,
    expert_ids,
    capacity,
    routed_gate,
    routed_up,
    routed_down,
    shared_gate,
    shared_up,
    shared_down_t,
):
    gathered_gate, gathered_up, gathered_down = (
        lax.all_gather(shared_gate, "expert", axis=0, tiled=True),
        lax.all_gather(shared_up, "expert", axis=0, tiled=True),
        lax.all_gather(shared_down_t, "expert", axis=0, tiled=True),
    )
    placement, route_weight = routing_tables(affinity, expert_ids, capacity)
    placement_half = placement.astype(jnp.bfloat16)
    outgoing = jnp.einsum(
        "ect,td->ecd", placement_half, tokens, preferred_element_type=jnp.float32
    ).astype(jnp.bfloat16)
    received = lax.all_to_all(outgoing, "expert", split_axis=0, concat_axis=0, tiled=True)
    flat_rows = received.reshape(-1, received.shape[-1])
    gate_rows = jnp.dot(flat_rows, routed_gate[0], preferred_element_type=jnp.float32)
    up_rows = jnp.dot(flat_rows, routed_up[0], preferred_element_type=jnp.float32)
    activated = (jax.nn.silu(gate_rows) * up_rows).astype(jnp.bfloat16)
    partial_out = jnp.dot(activated, routed_down[0], preferred_element_type=jnp.float32)
    partial_out = partial_out.reshape(received.shape[0], received.shape[1], partial_out.shape[-1])
    owner_total = lax.psum_scatter(
        partial_out.astype(jnp.bfloat16), "tensor", scatter_dimension=2, tiled=True
    ).astype(jnp.float32)
    back_rows = lax.all_to_all(
        owner_total.astype(jnp.bfloat16), "expert", split_axis=0, concat_axis=0, tiled=True
    ).astype(owner_total.dtype)
    shared_gate_rows = jnp.dot(tokens, gathered_gate, preferred_element_type=jnp.float32)
    shared_up_rows = jnp.dot(tokens, gathered_up, preferred_element_type=jnp.float32)
    shared_hidden = (jax.nn.silu(shared_gate_rows) * shared_up_rows).astype(jnp.bfloat16)
    shared_out = lax.dot_general(
        shared_hidden, gathered_down, (((1,), (1,)), ((), ())), preferred_element_type=jnp.float32
    )
    weighted = placement * route_weight.T[:, None, :]
    routed_out = jnp.einsum("ect,ecd->td", weighted, back_rows, precision=lax.Precision.HIGHEST)
    summed = lax.psum_scatter(
        shared_out.astype(jnp.bfloat16), "tensor", scatter_dimension=1, tiled=True
    ).astype(jnp.float32)
    mixed_out = summed + routed_out
    return mixed_out.astype(jnp.bfloat16)


SEMAPHORES = 64
VMEM_BYTES = 67043328
RING = 4
MESH = pl.DeviceIdType.MESH
F32 = jnp.float32
BF16 = jnp.bfloat16


def remote(src, dst, send_sem, recv_sem, **device):
    return pltpu.make_async_remote_copy(
        src_ref=src,
        dst_ref=dst,
        send_sem=send_sem,
        recv_sem=recv_sem,
        device_id=device,
        device_id_type=MESH,
    )


def fused_kernel(
    n_exp, n_ten,
    tok_any, aff_ref, ids_ref, cap_ref, rg_any, ru_any, rd_any, sg_any, su_any, sd_any,
    out_ref,
    tok, wgu, wdn, rgw, ruw, rdw, xall, xrel, gown, gpart, gsend, gin, hall, weights,
    rout, rin, ys, yin, yb, back, acc, osend, oin, xsend, xin, fsend, rfin, routed,
    lsem, ssem, rsem, cs, cr, xs, xr, fs, fr,
):
    e, t = lax.axis_index("expert"), lax.axis_index("tensor")
    core = lax.rem(t, 2)
    partner = t + 1 - 2 * core
    rows, width = tok.shape
    cols = width // n_exp
    half = rows // 2
    half_width = width // 2
    hidden = hall.shape[2]
    others = range(1, n_exp)
    started = []

    def link(src, dst, **device):
        at = len(started)
        copy = remote(src, dst, ssem.at[at], rsem.at[at], **device)
        copy.start()
        started.append(copy)
        return copy

    def up(k):
        return lax.rem(e + k + n_exp, n_exp)

    def span(index, size, unit=128):
        return pl.ds(pl.multiple_of(index * size, unit), size)

    right, left, opposite = up(1), up(-1), up(n_exp // 2)

    loads = [
        pltpu.make_async_copy(tok_any, tok, lsem.at[0]),
        pltpu.make_async_copy(sg_any, wgu.at[:, pl.ds(0, hidden)], lsem.at[1]),
        pltpu.make_async_copy(su_any, wgu.at[:, pl.ds(hidden, hidden)], lsem.at[2]),
        pltpu.make_async_copy(rg_any.at[0], rgw, lsem.at[3]),
        pltpu.make_async_copy(ru_any.at[0], ruw, lsem.at[4]),
        pltpu.make_async_copy(rd_any.at[0], rdw, lsem.at[5]),
        pltpu.make_async_copy(sd_any, wdn, lsem.at[6]),
    ]
    loads[0].start()

    barrier = pltpu.get_barrier_semaphore()
    for i in range(n_exp):
        for j in range(n_ten):
            if i or j:
                pl.semaphore_signal(
                    barrier,
                    inc=1,
                    device_id={"expert": up(i), "tensor": lax.rem(t + j, n_ten)},
                    device_id_type=MESH,
                )
    pl.semaphore_wait(barrier, n_exp * n_ten - 1)

    loads[0].wait()
    mine = span(core, half, 16)
    large = (cols // 128 + 1) // 2 * 128
    ahead, behind = up(1 - 2 * core), up(2 * core - 1)
    x_copy = {}
    for name, to in (("left", right), ("right", left)):
        x_copy[name] = link(
            tok.at[mine, span(to, cols)], xall.at[e, mine, :], expert=to
        )
    first = pl.multiple_of(opposite * cols, 128)
    x_large = link(
        tok.at[mine, pl.ds(first, large)], xrel.at[:, pl.ds(0, large)], expert=ahead
    )
    x_small = link(
        tok.at[mine, pl.ds(first + large, cols - large)],
        xrel.at[:, pl.ds(large, cols - large)],
        expert=behind,
    )

    for load in loads[1:]:
        load.start()

    lanes = n_exp * CAP
    line = lax.broadcasted_iota(jnp.int32, (lanes, rows), 0)
    expert_of, level = line // CAP, lax.rem(line, CAP)
    ids, aff = ids_ref[...], aff_ref[...]
    hit = jnp.zeros((lanes, rows), F32)
    chosen = jnp.zeros((lanes, rows), F32)
    for k in range(ids.shape[0]):
        match = (ids[k : k + 1, :] == expert_of).astype(F32)
        hit += match
        chosen += match * aff[k : k + 1, :]
    share = 2.5 * chosen / jnp.sum(aff, axis=0, keepdims=True)
    earlier = (
        lax.broadcasted_iota(jnp.int32, (rows, rows), 0)
        < lax.broadcasted_iota(jnp.int32, (rows, rows), 1)
    ).astype(BF16)
    slot = jnp.dot(hit.astype(BF16), earlier, preferred_element_type=F32)
    limit = jnp.zeros((lanes, rows), jnp.int32)
    for k in range(n_exp):
        limit = jnp.where(expert_of == k, cap_ref[k], limit)
    placed = (
        hit * (slot < limit.astype(F32)).astype(F32) * (slot == level.astype(F32)).astype(F32)
    )
    weights[...] = jnp.transpose(placed * share)
    chosen_rows = jnp.dot(placed.astype(BF16), tok[...], preferred_element_type=F32)
    for k in range(n_exp):
        rout[k] = chosen_rows[k * CAP : (k + 1) * CAP].astype(BF16)
    rin[e] = rout[e]

    x_pass = {}
    for name, index in (("left", left), ("right", right)):
        x_copy[name].wait_recv()
        x_pass[name] = link(
            xall.at[index, mine, :], xall.at[index, mine, :], tensor=partner
        )
    x_large.wait_recv()
    whole_large = xall.at[behind, mine, pl.ds(0, large)]
    x_large = link(xrel.at[:, pl.ds(0, large)], whole_large, expert=ahead)
    x_small.wait_recv()
    whole_small = xall.at[ahead, mine, pl.ds(large, cols - large)]
    x_small = link(xrel.at[:, pl.ds(large, cols - large)], whole_small, expert=behind)
    loads[1].wait()
    loads[2].wait()

    lower, upper = pl.ds(0, hidden), pl.ds(hidden, hidden)

    def project(index):
        return jnp.dot(xall[index], wgu[...], preferred_element_type=F32)

    x_pass["left"].wait_recv()
    found = project(left)
    gsend[0] = found[:, :hidden].astype(BF16)
    gpart[0] = found[:, hidden:]
    g_left = link(gsend.at[0], gin.at[0], expert=left)
    x_pass["right"].wait_recv()
    found = project(right)
    gsend[1] = found[:, hidden:].astype(BF16)
    gpart[1] = found[:, :hidden]
    g_right = link(gsend.at[1], gin.at[1], expert=right)

    side = span(core, half_width)
    b_copy = {}
    for k in others:
        b_copy[k] = link(rout.at[up(k), :, side], rin.at[e, :, side], expert=up(k))

    x_large.wait_recv()
    x_small.wait_recv()
    x_far = link(
        xall.at[opposite, mine, :], xall.at[opposite, mine, :], tensor=partner
    )
    x_far.wait_recv()
    found = project(opposite)
    gsend[2] = found[:, :hidden].astype(BF16)
    g_low = link(gsend.at[2], gin.at[2], expert=right)
    gsend[3] = found[:, hidden:].astype(BF16)
    g_high = link(gsend.at[3], gin.at[3], expert=left)
    gown[...] = jnp.dot(tok[:, span(e, cols)], wgu[...], preferred_element_type=F32)
    b_pass = {}
    for k in others:
        b_copy[k].wait_recv()
        b_pass[k] = link(
            rin.at[up(-k), :, side], rin.at[up(-k), :, side], tensor=partner
        )
    g_low.wait_recv()
    gsend[4] = (gpart[1] + gin[2].astype(F32)).astype(BF16)
    g_low = link(gsend.at[4], gin.at[4], expert=right)
    g_high.wait_recv()
    gsend[5] = (gpart[0] + gin[3].astype(F32)).astype(BF16)
    g_high = link(gsend.at[5], gin.at[5], expert=left)

    g_left.wait_recv()
    g_right.wait_recv()
    g_low.wait_recv()
    g_high.wait_recv()
    gate = gown[:, :hidden] + gin[0].astype(F32) + gin[4].astype(F32)
    above = gown[:, hidden:] + gin[1].astype(F32) + gin[5].astype(F32)
    hall[e] = (gate * (1.0 / (1.0 + jnp.exp(-gate))) * above).astype(BF16)
    near, far = pl.ds(0, hidden // 2), pl.ds(hidden // 2, hidden // 2)
    from_left = link(hall.at[e, :, near], hall.at[e, :, near], expert=right)
    from_right = link(hall.at[e, :, far], hall.at[e, :, far], expert=left)
    rest_left = link(hall.at[e, :, far], hall.at[e, :, far], expert=right)
    rest_right = link(hall.at[e, :, near], hall.at[e, :, near], expert=left)

    for load in loads[3:]:
        load.wait()
    for k in others:
        b_pass[k].wait_recv()
    flat = jnp.concatenate([rin[k].astype(F32) for k in range(n_exp)], axis=0).astype(BF16)
    gate = jnp.dot(flat, rgw[...], preferred_element_type=F32)
    above = jnp.dot(flat, ruw[...], preferred_element_type=F32)
    act = (gate * (1.0 / (1.0 + jnp.exp(-gate))) * above).astype(BF16)
    from_left.wait_recv()
    from_left = link(hall.at[left, :, near], hall.at[left, :, near], expert=right)
    from_right.wait_recv()
    from_right = link(hall.at[right, :, far], hall.at[right, :, far], expert=left)
    ys[...] = jnp.dot(act, rdw[...], preferred_element_type=F32).astype(BF16)
    y_copy = {}
    part = width // n_ten
    for k in range(1, n_ten):
        to = lax.rem(t + k, n_ten)
        y_copy[k] = link(ys.at[:, span(to, part)], yin.at[k - 1], tensor=to)

    k_at = len(started)

    def k_copy(k):
        return remote(
            yb.at[up(k)], back.at[e], ssem.at[k_at + k - 1], rsem.at[k_at + k - 1], expert=up(k)
        )

    def join_routed():
        total = ys[:, span(t, part)].astype(F32)
        for k in range(1, n_ten):
            y_copy[k].wait_recv()
            total = total + yin[k - 1].astype(F32)
        for k in range(n_exp):
            yb[k] = total[k * CAP : (k + 1) * CAP].astype(BF16)
        back[e] = yb[e]
        for k in others:
            k_copy(k).start()

    def product(index):
        return lax.dot_general(
            hall[index], wdn[...], (((1,), (1,)), ((), ())), preferred_element_type=F32
        )

    x_bit = t // 2
    x_peer = lax.rem(t + 2, n_ten)
    keep_half, give_half = span(x_bit, half, 16), span(1 - x_bit, half, 16)
    blocks = [e, left, right, opposite]
    arrivals = [[], [rest_left], [rest_right], [from_left, from_right]]

    def core_copy(j):
        return remote(osend.at[j], oin.at[j], cs.at[j], cr.at[j], tensor=partner)

    def x_copy_of(j):
        return remote(xsend.at[j], xin.at[j], xs.at[j], xr.at[j], tensor=x_peer)

    def last_copy(j):
        return remote(
            fsend.at[j], rfin.at[keep_half, :], fs.at[j], fr.at[x_bit],
            expert=blocks[j], tensor=e,
        )

    def compute(j):
        for copy in arrivals[j]:
            copy.wait_recv()
        return product(blocks[j])

    def give(j):
        osend[j] = compute(j).astype(BF16)
        core_copy(j).start()

    def take(j):
        acc[j] = compute(j)
        core_copy(j).wait_recv()
        xsend[j] = (acc[j, give_half, :] + oin[j, give_half, :].astype(F32)).astype(BF16)
        x_copy_of(j).start()

    def finish(j):
        both = acc[j, keep_half, :] + oin[j, keep_half, :].astype(F32)
        x_copy_of(j).wait_recv()
        value = (both + xin[j].astype(F32)).astype(BF16)
        if j:
            fsend[j] = value
            last_copy(j).start()
        else:

            @pl.when(e == t)
            def _():
                rfin[keep_half, :] = value

            @pl.when(e != t)
            def _():
                fsend[j] = value
                last_copy(j).start()

    def settle(kept, given):
        for j in given:
            core_copy(j).wait_send()
        for j in kept:
            x_copy_of(j).wait_send()
            if j:
                last_copy(j).wait_send()
            else:

                @pl.when(e != t)
                def _():
                    last_copy(j).wait_send()

    even = lax.rem(e + core, 2) == 0

    @pl.when(even)
    def _():
        take(0)
        give(1)
        give(2)
        finish(0)
        join_routed()
        take(3)
        finish(3)
        settle((0, 3), (1, 2))

    @pl.when(jnp.logical_not(even))
    def _():
        give(0)
        take(1)
        take(2)
        finish(1)
        finish(2)
        give(3)
        join_routed()
        settle((1, 2), (0, 3))

    for k in others:
        k_copy(k).wait()
    rows_back = jnp.concatenate([back[k].astype(F32) for k in range(n_exp)], axis=0)
    routed[...] = jnp.dot(
        weights[...], rows_back, preferred_element_type=F32, precision=lax.Precision.HIGHEST
    )

    for h in range(2):

        @pl.when(jnp.logical_or(e != t, x_bit != h))
        def _():
            remote(
                fsend.at[0], rfin.at[pl.ds(h * half, half), :], fs.at[0], fr.at[h],
                expert=t, tensor=e,
            ).wait_recv()

    out_ref[...] = (rfin[...].astype(F32) + routed[...]).astype(BF16)
    for copy in started:
        copy.wait_send()


def fused(n_exp, n_ten, *args):
    tokens, affinity, expert_ids, capacity, rg, ru, rd, sg, su, sd = args
    rows, width = tokens.shape
    hidden = sg.shape[1]
    cols, part = width // n_exp, width // n_ten
    any_spec = pl.BlockSpec(memory_space=pl.ANY)
    vmem = pl.BlockSpec(memory_space=pltpu.VMEM)
    scratch = [
        pltpu.VMEM((rows, width), BF16),
        pltpu.VMEM((cols, 2 * hidden), BF16),
        pltpu.VMEM((cols, hidden), BF16),
        pltpu.VMEM(rg.shape[1:], BF16),
        pltpu.VMEM(ru.shape[1:], BF16),
        pltpu.VMEM(rd.shape[1:], BF16),
        pltpu.VMEM((n_exp, rows, cols), BF16),
        pltpu.VMEM((rows // 2, cols), BF16),
        pltpu.VMEM((rows, 2 * hidden), F32),
        pltpu.VMEM((2, rows, hidden), F32),
        pltpu.VMEM((6, rows, hidden), BF16),
        pltpu.VMEM((6, rows, hidden), BF16),
        pltpu.VMEM((n_exp, rows, hidden), BF16),
        pltpu.VMEM((rows, n_exp * CAP), F32),
        pltpu.VMEM((n_exp, CAP, width), BF16),
        pltpu.VMEM((n_exp, CAP, width), BF16),
        pltpu.VMEM((n_exp * CAP, width), BF16),
        pltpu.VMEM((n_ten - 1, n_exp * CAP, part), BF16),
        pltpu.VMEM((n_exp, CAP, part), BF16),
        pltpu.VMEM((n_exp, CAP, part), BF16),
        pltpu.VMEM((n_exp, rows, part), F32),
        pltpu.VMEM((n_exp, rows, part), BF16),
        pltpu.VMEM((n_exp, rows, part), BF16),
        pltpu.VMEM((n_exp, rows // 2, part), BF16),
        pltpu.VMEM((n_exp, rows // 2, part), BF16),
        pltpu.VMEM((n_exp, rows // 2, part), BF16),
        pltpu.VMEM((rows, part), BF16),
        pltpu.VMEM((rows, part), F32),
        pltpu.SemaphoreType.DMA((7,)),
        pltpu.SemaphoreType.DMA((SEMAPHORES,)),
        pltpu.SemaphoreType.DMA((SEMAPHORES,)),
    ]
    scratch += [pltpu.SemaphoreType.DMA((n_exp,))] * 5 + [pltpu.SemaphoreType.DMA((2,))]
    return pl.pallas_call(
        functools.partial(fused_kernel, n_exp, n_ten),
        out_shape=jax.ShapeDtypeStruct((rows, part), BF16),
        in_specs=[any_spec, vmem, vmem, pl.BlockSpec(memory_space=pltpu.SMEM)] + [any_spec] * 6,
        out_specs=vmem,
        scratch_shapes=scratch,
        compiler_params=pltpu.CompilerParams(
            collective_id=0, has_side_effects=True, vmem_limit_bytes=VMEM_BYTES
        ),
    )(tokens, affinity.T, expert_ids.T, *args[3:])


def fits(n_exp, n_ten, tokens, capacity, routed_gate, shared_gate):
    rows, width = tokens.shape
    return (
        n_exp == RING
        and n_ten == n_exp
        and capacity.shape[0] == n_exp
        and routed_gate.shape[0] == 1
        and rows % 32 == 0
        and width % 256 == 0
        and width // n_exp >= 256
        and width % (128 * n_exp) == 0
        and shared_gate.shape[1] % 256 == 0
    )


def layer(n_exp, n_ten, *args):
    if fits(n_exp, n_ten, args[0], args[3], args[4], args[7]):
        return fused(n_exp, n_ten, *args)
    return local(*args)


def solution(mesh):
    in_specs = (
        P(("groups", "expert"), None),
        P(("groups", "expert"), None),
        P(("groups", "expert"), None),
        P("groups"),
        P("expert", None, "tensor"),
        P("expert", None, "tensor"),
        P("expert", "tensor", None),
        P("expert", "tensor"),
        P("expert", "tensor"),
        P("expert", "tensor"),
    )
    out_specs = P(("groups", "expert"), "tensor")
    body = functools.partial(layer, mesh.shape["expert"], mesh.shape["tensor"])
    return jax.shard_map(body, mesh=mesh, in_specs=in_specs, out_specs=out_specs, check_vma=False)
```
